512 devices in a mesh: blk: 32 (over y, z_hi, core), sub: 16 (over z_lo, x).
Axes of the slice: x: 4, y: 4, z: 16 (z_hi: 4, z_lo: 4; z = z_hi * 4 + z_lo), core: 2. Of those that a mesh axis runs over, the one named last changes fastest.
Arguments:
- features: float32 [16384, 512], P(('blk', 'sub')), may hold values from -3 to 3
- lengthscale: float32 [512], replicated, may hold values from 0.7 to 1.4
- probes: float32 [16384, 64], P(('blk', 'sub')), may hold values from -6 to 6
- cotangent: float32 [16384, 64], P(('blk', 'sub')), may hold values from -1.5 to 1.5
Outputs:
- product: float32 [16384, 64], P(('blk', 'sub'))
- scaled_grad: float32 [16384, 512], P(('blk', 'sub'))
The draws below stay inside these ranges and needn't reach their ends.
All inputs are finite; a program needn't handle non-finite values.
Results may differ from the reference program's by a relative error of at most 0.0003.
Values sent between devices are 32-bit elements; how exact they have to be, the bound alone decides.
A program may use at most 64 MiB of HBM per device.

```python
import math
import jax
import jax.numpy as jnp
from jax import lax

F = 512
P_SIZE = 64
NB = 512
NPTS = 16384
N_BLK = 32


latent_count = 8


def draw_features(key, part):
    key_latent = jax.random.fold_in(key, 101)
    key_mixing = jax.random.fold_in(key, 202)
    key_noise = jax.random.fold_in(key, 303)
    latent = jnp.clip(jax.random.normal(key_latent, (NPTS, latent_count), jnp.float32), -4.0, 4.0)
    row_scale = jnp.ones((NPTS, 1), jnp.float32)
    mixing = jnp.clip(jax.random.normal(key_mixing, (latent_count, F), jnp.float32), -4.0, 4.0) / math.sqrt(F)
    noise = jnp.clip(jax.random.normal(key_noise, (NPTS, F), jnp.float32), -4.0, 4.0) * (row_scale / math.sqrt(F))
    mapped = jnp.dot(latent, mixing, precision=lax.Precision.HIGHEST, preferred_element_type=jnp.float32)
    return jnp.clip(mapped + noise, -3.0, 3.0).astype(jnp.float32)


def shard_levels(stream_key, extent, shards, low, largest):
    factor_of = 1.0
    for dim, parts in shards:
        draws = jax.random.uniform(jax.random.fold_in(jax.random.fold_in(stream_key, 6), dim), (parts,), jnp.float32, low / len(shards), largest / len(shards))
        factor_of = factor_of * jnp.repeat(jnp.exp(draws), extent[dim] // parts).reshape((-1,) + (1,) * (len(extent) - 1 - dim))
    return factor_of


def bell_draw(key, extent, width, most, pieces=(), kind=jnp.bfloat16):
    drawn = jax.random.normal(key, extent, jnp.float32) * width
    if len(pieces) > 0:
        drawn = shard_levels(key, extent, pieces, -0.22, 0.18) * drawn
    return jnp.clip(drawn, min=-most, max=most).astype(kind)


def setup_inputs(seed: int = 0) -> dict:
    splits = jax.random.split(jax.random.key(seed), 5)
    return {
        "features": draw_features(jax.random.fold_in(splits[4], 71), 0),
        "lengthscale": jnp.clip(jnp.exp(jax.random.uniform(splits[1], (F,), jnp.float32, math.log(0.7), math.log(1.4))), 0.7, 1.4),
        "probes": bell_draw(splits[2], (NPTS, P_SIZE), 1.0, 6.0, ((0, 512),), jnp.float32),
        "cotangent": bell_draw(splits[3], (NPTS, P_SIZE), 0.25, 1.5, ((0, 512),), jnp.float32),
    }


HIGH = lax.Precision.HIGHEST


def reference(features, lengthscale, probes, cotangent):
    scaled = features / lengthscale[None, :]
    norms = jnp.sum(scaled * scaled, axis=1)
    pairs = jnp.concatenate([probes, cotangent], axis=1)
    swapped = jnp.concatenate([cotangent, probes], axis=1)

    def one_block(inputs):
        block_scaled, block_norms, block_pairs = inputs
        inner = jnp.dot(block_scaled, scaled.T, precision=HIGH, preferred_element_type=jnp.float32)
        kernel = jnp.exp(-0.5 * (block_norms[:, None] + norms[None, :] - 2.0 * inner))
        cross = jnp.dot(block_pairs, swapped.T, precision=HIGH, preferred_element_type=jnp.float32)
        weight = kernel * cross
        block_product = jnp.dot(kernel, probes, precision=HIGH, preferred_element_type=jnp.float32)
        block_gradient = jnp.dot(weight, scaled, precision=HIGH, preferred_element_type=jnp.float32)
        block_gradient = block_gradient - jnp.sum(weight, axis=1)[:, None] * block_scaled
        return block_product, block_gradient

    product, gradient = lax.map(one_block, (scaled.reshape(N_BLK, NB, F), norms.reshape(N_BLK, NB), pairs.reshape(N_BLK, NB, 2 * P_SIZE)))
    return product.reshape(NPTS, P_SIZE), gradient.reshape(NPTS, F)
```

```python
import functools

import jax
import jax.numpy as jnp
from jax import lax
from jax.experimental import pallas as pl
from jax.experimental.pallas import tpu as pltpu
from jax.sharding import PartitionSpec as P

BF = jnp.bfloat16
F32 = jnp.float32
NT = (((1,), (1,)), ((), ()))
NN = (((1,), (0,)), ((), ()))
MESH = pl.DeviceIdType.MESH

OWN = 32
W = 640
CHIPS_Z = 16
PLANE = 4


def place():
    blk, sub = lax.axis_index("blk"), lax.axis_index("sub")
    core = lax.rem(blk, 2)
    z = lax.rem(lax.div(blk, 2), 4) * 4 + lax.div(sub, 4)
    y = lax.div(blk, 8)
    x = lax.rem(sub, 4)
    return x, y, z, core


def device(x, y, z, core):
    return (y * 8 + lax.div(z, 4) * 2 + core, lax.rem(z, 4) * 4 + x)


def peers():
    x, y, z, core = place()
    along_x = [None] + [device(lax.rem(x + k, 4), y, z, core) for k in (1, 2, 3)]
    along_y = [None] + [device(x, lax.rem(y + k, 4), z, core) for k in (1, 2, 3)]
    up = device(x, y, lax.rem(z + 1, CHIPS_Z), core)
    down = device(x, y, lax.rem(z + CHIPS_Z - 1, CHIPS_Z), core)
    partner = device(x, y, z, 1 - core)
    return along_x, along_y, up, down, partner


def meet(devices):
    barrier = pltpu.get_barrier_semaphore()
    for d in devices:
        pl.semaphore_signal(barrier, inc=1, device_id=d, device_id_type=MESH)
    pl.semaphore_wait(barrier, len(devices))


def copy_to(src, dst, send, recv, to):
    return pltpu.make_async_remote_copy(
        src_ref=src, dst_ref=dst, send_sem=send, recv_sem=recv, device_id=to, device_id_type=MESH
    )


def gather_kernel(f_ref, ls_ref, pr_ref, ct_ref, rows_ref, line_ref, zs, zr, ks, kr, as_, ar, bs, br):
    along_x, along_y, up, down, partner = peers()
    own = f_ref[...] / ls_ref[...]
    line_ref[0, 0, :, 0:512] = own
    line_ref[0, 0, :, 512:576] = pr_ref[...]
    line_ref[0, 0, :, 576:640] = ct_ref[...]
    for h in range(2):
        part = slice(h * 16, h * 16 + 16)
        rows_ref[h, 0, 0, :, 0:512] = own[part]
        rows_ref[h, 0, 0, :, 512:576] = pr_ref[part, :]
        rows_ref[h, 0, 0, :, 576:640] = ct_ref[part, :]
    meet(along_x[1:] + along_y[1:] + [up, down, partner])

    def z_copy(way, s, q):
        src = s if way == 0 else (CHIPS_Z - s if not isinstance(s, int) or s else 0)
        dst = s + 1 if way == 0 else CHIPS_Z - 1 - s
        rows = pl.ds(8 * q, 8)
        return copy_to(
            line_ref.at[0, src, rows], line_ref.at[0, dst, rows],
            zs.at[way, s, q], zr.at[way, s, q], (up, down)[way],
        )

    def k_copy(slot):
        return copy_to(line_ref.at[0, slot], line_ref.at[1, slot], ks.at[slot], kr.at[slot], partner)

    def a_first(k):
        return copy_to(rows_ref.at[0, 0, 0], rows_ref.at[0, 0, 4 - k], as_.at[0, k], ar.at[0, k], along_x[k])

    def a_then(dx, k):
        return copy_to(rows_ref.at[0, 0, dx], rows_ref.at[0, 4 - k, dx], as_.at[1 + dx, k], ar.at[1 + dx, k], along_y[k])

    def b_first(k):
        return copy_to(rows_ref.at[1, 0, 0], rows_ref.at[1, 4 - k, 0], bs.at[0, k], br.at[0, k], along_y[k])

    def b_then(dy, k):
        return copy_to(rows_ref.at[1, dy, 0], rows_ref.at[1, dy, 4 - k], bs.at[1 + dy, k], br.at[1 + dy, k], along_x[k])

    for q in range(4):
        z_copy(0, 0, q).start()
        z_copy(1, 0, q).start()
    for k in (1, 3, 2):
        a_first(k).start()
        b_first(k).start()
    k_copy(0).start()
    for k in (1, 3, 2):
        a_then(0, k).start()
        b_then(0, k).start()

    def z_step(s):
        for q in range(4):
            for way in range(2):
                z_copy(way, s - 1, q).wait_recv()
                z_copy(way, s, q).start()
        k_copy(s).start()
        k_copy(CHIPS_Z - s).start()

    z_step(1)
    for k in (1, 3, 2):
        a_first(k).wait_recv()
        for j in (1, 3, 2):
            a_then(4 - k, j).start()
        b_first(k).wait_recv()
        for j in (1, 3, 2):
            b_then(4 - k, j).start()

    def body(s, carry):
        z_step(s)
        return carry

    lax.fori_loop(2, 7, body, 0)
    for q in range(4):
        for way in range(2):
            z_copy(way, 6, q).wait_recv()
            if q // 2 == way:
                z_copy(way, 7, q).start()
    k_copy(7).start()
    k_copy(9).start()
    for way in range(2):
        for q in (2 * way, 2 * way + 1):
            z_copy(way, 7, q).wait_recv()
    k_copy(8).start()

    for dx in range(4):
        for k in (1, 2, 3):
            a_then(dx, k).wait_recv()
            b_then(dx, k).wait_recv()
    for slot in range(16):
        k_copy(slot).wait()
    for k in (1, 2, 3):
        a_first(k).wait_send()
        b_first(k).wait_send()
        for dx in range(4):
            a_then(dx, k).wait_send()
            b_then(dx, k).wait_send()

    def drain(s, carry):
        for q in range(4):
            for way in range(2):
                z_copy(way, s, q).wait_send()
        return carry

    for q in range(4):
        for way in range(2):
            z_copy(way, 0, q).wait_send()
    lax.fori_loop(1, 7, drain, 0)
    for way in range(2):
        for q in (2 * way, 2 * way + 1):
            z_copy(way, 7, q).wait_send()


def halves(x):
    high = x.astype(BF)
    return high, (x - high.astype(F32)).astype(BF)


def dot(a, b, dims):
    return lax.dot_general(a, b, dims, preferred_element_type=F32)


COLS = 256
ROWS = 512


def pair_kernel(rows_ref, line_ref, out_ref, row_parts, pair_parts, row_norms, col_parts, swapped, col_stack, probe_stack):
    n_rows = rows_ref.shape[0]
    n_cols = line_ref.shape[0]

    def prepare(r, carry):
        rows = pl.ds(pl.multiple_of(r * 128, 128), 128)
        x = rows_ref[rows, 0:512]
        high, low = halves(x)
        row_parts[0, rows, :] = high
        row_parts[1, rows, :] = low
        row_norms[rows, :] = jnp.broadcast_to(0.5 * jnp.sum(x * x, axis=1, keepdims=True), (128, 128))
        high, low = halves(rows_ref[rows, 512:640])
        pair_parts[rows, 0:128] = high
        pair_parts[rows, 128:256] = low
        out_ref[rows, :] = jnp.zeros((128, W), F32)
        return carry

    lax.fori_loop(0, n_rows // 128, prepare, 0)

    def chunk(c, carry):
        cols = pl.ds(pl.multiple_of(c * COLS, COLS), COLS)
        x = line_ref[cols, 0:512]
        high, low = halves(x)
        col_parts[0:COLS, :] = high
        col_parts[COLS : 2 * COLS, :] = low
        square = x * x
        folded = square[:, 0:128] + square[:, 128:256] + square[:, 256:384] + square[:, 384:512]
        col_norms = 0.5 * jnp.sum(folded.T, axis=0, keepdims=True)
        pr_high, pr_low = halves(line_ref[cols, 512:576])
        ct_high, ct_low = halves(line_ref[cols, 576:640])
        for k, (ct, pr) in enumerate(((ct_high, pr_high), (ct_low, pr_low))):
            for at in (0, 128):
                swapped[k * COLS : (k + 1) * COLS, at : at + 64] = ct
                swapped[k * COLS : (k + 1) * COLS, at + 64 : at + 128] = pr
        for k, part in enumerate((high, high, low)):
            col_stack[k * COLS : (k + 1) * COLS, :] = part
        for k in range(2):
            probe_stack[k * COLS : (k + 1) * COLS, 0:64] = pr_high
            probe_stack[k * COLS : (k + 1) * COLS, 64:128] = pr_low

        def block(r, carry):
            rows = pl.ds(pl.multiple_of(r * ROWS, ROWS), ROWS)
            both = col_parts[...]
            a = dot(row_parts[0, rows, :], both, NT) + dot(row_parts[1, rows, :], both, NT)
            inner = a[:, 0:COLS] + a[:, COLS : 2 * COLS]
            b = dot(pair_parts[rows, :], swapped[...], NT)
            cross = b[:, 0:COLS] + b[:, COLS : 2 * COLS]
            norms = row_norms[rows, :]
            norms = jnp.concatenate([norms] * (COLS // 128), axis=1)
            kernel = jnp.exp(inner - norms - col_norms)
            weight = kernel * cross
            k_high, k_low = halves(kernel)
            w_high, w_low = halves(weight)
            gradient = dot(jnp.concatenate([w_high, w_low, w_high], axis=1), col_stack[...], NN)
            product = dot(jnp.concatenate([k_high, k_low], axis=1), probe_stack[...], NN)
            out_ref[rows, 0:512] += gradient
            sums = jnp.sum(weight, axis=1, keepdims=True)
            out_ref[rows, 512:640] += jnp.concatenate(
                [product[:, 0:64] + product[:, 64:128], jnp.broadcast_to(sums, (ROWS, 64))], axis=1
            )
            return carry

        lax.fori_loop(0, n_rows // ROWS, block, 0)
        return carry

    lax.fori_loop(0, n_cols // COLS, chunk, 0)


def scatter_kernel(part_ref, f_ref, ls_ref, product_ref, gradient_ref, a1, b1, at, bt, a2, b2, ss, sr):
    along_x, along_y, _, _, _ = peers()
    meet(along_x[1:] + along_y[1:])

    def a_first(k):
        return copy_to(part_ref.at[0, :, k], a1.at[k - 1], ss.at[0, k], sr.at[0, k], along_x[k])

    def b_first(k):
        return copy_to(part_ref.at[1, k], b1.at[k - 1], ss.at[1, k], sr.at[1, k], along_y[k])

    def a_then(k):
        return copy_to(at.at[k], a2.at[k - 1], ss.at[2, k], sr.at[2, k], along_y[k])

    def b_then(k):
        return copy_to(bt.at[k], b2.at[k - 1], ss.at[3, k], sr.at[3, k], along_x[k])

    for k in (1, 3, 2):
        a_first(k).start()
        b_first(k).start()
    for k in (1, 2, 3):
        a_first(k).wait_recv()
        b_first(k).wait_recv()
    for j in (1, 3, 2, 0):
        at[j] = part_ref[0, j, 0] + a1[0, j] + a1[1, j] + a1[2, j]
        bt[j] = part_ref[1, 0, j] + b1[0, j] + b1[1, j] + b1[2, j]
        if j:
            a_then(j).start()
            b_then(j).start()
    for k in (1, 2, 3):
        a_then(k).wait_recv()
        b_then(k).wait_recv()
    for h, (t, u) in enumerate(((at, a2), (bt, b2))):
        rows = slice(16 * h, 16 * h + 16)
        total = t[0] + u[0] + u[1] + u[2]
        scaled = f_ref[rows, :] / ls_ref[...]
        product_ref[rows, :] = total[:, 512:576]
        gradient_ref[rows, :] = total[:, 0:512] - total[:, 576:577] * scaled
    for k in (1, 2, 3):
        for c in (a_first, b_first, a_then, b_then):
            c(k).wait_send()


VMEM = pl.BlockSpec(memory_space=pltpu.VMEM)
DMA = pltpu.SemaphoreType.DMA


def on_device(features, lengthscale, probes, cotangent):
    scale = lengthscale[None, :]
    rows, line = pl.pallas_call(
        gather_kernel,
        out_shape=(
            jax.ShapeDtypeStruct((2, 4, 4, 16, W), F32),
            jax.ShapeDtypeStruct((2, 16, OWN, W), F32),
        ),
        in_specs=[VMEM] * 4,
        out_specs=(VMEM, VMEM),
        scratch_shapes=[
            DMA((2, 8, 4)), DMA((2, 8, 4)), DMA((16,)), DMA((16,)),
            DMA((5, 4)), DMA((5, 4)), DMA((5, 4)), DMA((5, 4)),
        ],
        compiler_params=pltpu.CompilerParams(collective_id=0, has_side_effects=True),
        name="gather",
    )(features, scale, probes, cotangent)
    part = pl.pallas_call(
        pair_kernel,
        out_shape=jax.ShapeDtypeStruct((512, W), F32),
        in_specs=[VMEM] * 2,
        out_specs=VMEM,
        scratch_shapes=[
            pltpu.VMEM((2, 512, 512), BF), pltpu.VMEM((512, 256), BF), pltpu.VMEM((512, 128), F32),
            pltpu.VMEM((2 * COLS, 512), BF), pltpu.VMEM((2 * COLS, 256), BF),
            pltpu.VMEM((3 * COLS, 512), BF), pltpu.VMEM((2 * COLS, 128), BF),
        ],
        name="pairs",
    )(rows.reshape(512, W), line.reshape(1024, W))
    return pl.pallas_call(
        scatter_kernel,
        out_shape=(jax.ShapeDtypeStruct(probes.shape, F32), jax.ShapeDtypeStruct(features.shape, F32)),
        in_specs=[VMEM] * 3,
        out_specs=(VMEM, VMEM),
        scratch_shapes=[
            pltpu.VMEM((3, 4, 16, W), F32), pltpu.VMEM((3, 4, 16, W), F32),
            pltpu.VMEM((4, 16, W), F32), pltpu.VMEM((4, 16, W), F32),
            pltpu.VMEM((3, 16, W), F32), pltpu.VMEM((3, 16, W), F32),
            DMA((4, 4)), DMA((4, 4)),
        ],
        compiler_params=pltpu.CompilerParams(collective_id=1, has_side_effects=True),
        name="scatter",
    )(part.reshape(2, 4, 4, 16, W), features, scale)


def solution(mesh):
    spec = P(("blk", "sub"), None)
    return jax.shard_map(
        on_device, mesh=mesh, in_specs=(spec, P(), spec, spec), out_specs=(spec, spec), check_vma=False
    )
```
